32 devices in a mesh: fsdp: 8 (over z, y), tp: 4 (over x, core).
Axes of the slice: x: 2, y: 2, z: 4, core: 2. Of those that a mesh axis runs over, the one named last changes fastest.
Arguments:
- activations: bfloat16 [8192, 4096], P('fsdp', 'tp'), may hold values from -6 to 6
- out_grads: bfloat16 [2, 8192, 1024], P(None, 'fsdp', 'tp'), may hold values from -0.06591797 to 0.06591797
- bases: float32 [2, 4096, 256], P(None, 'fsdp'), may hold values from -0.09375 to 0.09375
- weights: float32 [2, 4096, 1024], P(None, 'fsdp', 'tp'), may hold values from -6 to 6
- first_moment: float32 [2, 256, 1024], P(None, 'fsdp', 'tp'), may hold values from -6 to 6
- second_moment: float32 [2, 256, 1024], P(None, 'fsdp', 'tp'), may hold values from 0.01 to 1
Outputs:
- new_weights: float32 [2, 4096, 1024], P(None, 'fsdp', 'tp')
- new_first: float32 [2, 256, 1024], P(None, 'fsdp', 'tp')
- new_second: float32 [2, 256, 1024], P(None, 'fsdp', 'tp')
- new_bases: float32 [2, 4096, 256], P(None, 'fsdp')
The draws below stay inside these ranges and needn't reach their ends.
All inputs are finite; a program needn't handle non-finite values.
Results may differ from the reference program's by a relative error of at most 0.0003.
Values may be sent and summed in bfloat16 or wider, within the bound.
A program may use at most 128 MiB of HBM per device.

```python
import math
import jax
import jax.numpy as jnp
from jax import lax

D = 4096
KV = 1024
RANK = 256
NS_STEPS = 5
TOKENS = 8192


def steps_of(stream_key, shape, cuts, smallest, largest):
    level = 1.0
    for position, blocks in cuts:
        draws = jax.random.uniform(jax.random.fold_in(jax.random.fold_in(stream_key, 6), position), (blocks,), jnp.float32, smallest / len(cuts), largest / len(cuts))
        level = level * jnp.repeat(jnp.exp(draws), shape[position] // blocks).reshape((-1,) + (1,) * (len(shape) - 1 - position))
    return level


def normal_values(key, dims, width, bound, shards=(), held_as=jnp.bfloat16):
    values = jax.random.normal(key, dims, jnp.float32) * width
    if len(shards) > 0:
        values = steps_of(key, dims, shards, -0.22, 0.18) * values
    return jnp.clip(values, min=-bound, max=bound).astype(held_as)


def setup_inputs(seed: int = 0) -> dict:
    key_list = jax.random.split(jax.random.key(seed), 7)
    return {
        "activations": normal_values(key_list[0], (TOKENS, D), 1.0, 6.0, ((0, 8), (1, 4))),
        "out_grads": normal_values(key_list[1], (2, TOKENS, KV), (1.0 / TOKENS ** 0.5), 0.06591797, ((1, 8), (2, 4))),
        "bases": normal_values(key_list[2], (2, D, RANK), D ** -0.5, 0.09375, ((1, 8),), jnp.float32),
        "weights": normal_values(key_list[3], (2, D, KV), 1.0, 6.0, ((1, 8), (2, 4)), jnp.float32),
        "first_moment": normal_values(key_list[4], (2, RANK, KV), 1.0, 6.0, ((1, 8), (2, 4)), jnp.float32),
        "second_moment": jnp.clip(jnp.exp(math.log(1.0) - 4.6051702 * jax.random.uniform(key_list[5], (2, RANK, KV), jnp.float32) ** steps_of(key_list[5], (2, RANK, KV), ((1, 8), (2, 4)), -0.2, 0.2)), 0.01, 1.0),
    }


COEF_A = 3.4445
COEF_B = -4.775
COEF_C = 2.0315
BETA_ONE = 0.9
BETA_TWO = 0.999
CORRECT_ONE = 1.0 - 0.9 ** 10
CORRECT_TWO = 1.0 - 0.999 ** 10
EPSILON = 1e-08
NORM_EPS = 1e-07
RATE = 2.0

def reference(activations, out_grads, bases, weights, first_moment, second_moment):
    high = lax.Precision.HIGHEST
    flipped = activations.T
    grads = jnp.stack([jnp.dot(flipped, out_grads[0], preferred_element_type=jnp.float32), jnp.dot(flipped, out_grads[1], preferred_element_type=jnp.float32)])
    projected = jnp.einsum('mdk,mdc->mkc', bases, grads, precision=high)
    new_first = BETA_ONE * first_moment + (1.0 - BETA_ONE) * projected
    new_second = BETA_TWO * second_moment + (1.0 - BETA_TWO) * projected * projected
    adam_step = new_first / CORRECT_ONE / (jnp.sqrt(new_second / CORRECT_TWO) + EPSILON)
    new_weights = weights - RATE * jnp.einsum('mdk,mkc->mdc', bases, adam_step, precision=high)
    candidate = jnp.einsum('mdc,mkc->mdk', grads, projected, precision=high)
    scale = jnp.sqrt(lax.optimization_barrier(jnp.sum(candidate * candidate, axis=(1, 2)))) + NORM_EPS
    current = candidate / scale[:, None, None]
    for step in range(NS_STEPS):
        gram = jnp.einsum('mdk,mdl->mkl', current, current, precision=high)
        mixer = COEF_B * gram + COEF_C * jnp.einsum('mkl,mlj->mkj', gram, gram, precision=high)
        current = COEF_A * current + jnp.einsum('mdk,mkl->mdl', current, mixer, precision=high)
    return (new_weights, new_first, new_second, current)
```

```python
import functools

import jax
import jax.numpy as jnp
from jax import lax
from jax.experimental import pallas as pl
from jax.experimental.pallas import tpu as pltpu
from jax.sharding import PartitionSpec as P

NS_STEPS = 5


COEF_A = 3.4445
COEF_B = -4.775
COEF_C = 2.0315
BETA_ONE = 0.9
BETA_TWO = 0.999
CORRECT_ONE = 1.0 - 0.9**10
CORRECT_TWO = 1.0 - 0.999**10
EPSILON = 1e-08
NORM_EPS = 1e-07
RATE = 2.0
HIGH = lax.Precision.HIGHEST
MESH = pl.DeviceIdType.MESH


def exchange_kernel(axis, count, scatter, x_ref, out_ref, own_sem, send_sem, recv_sem):
    me = lax.axis_index(axis)
    barrier = pltpu.get_barrier_semaphore()
    for hop in range(1, count):
        peer = lax.rem(me + hop, count)
        pl.semaphore_signal(barrier, inc=1, device_id={axis: peer}, device_id_type=MESH)
    own = pltpu.make_async_copy(x_ref.at[me] if scatter else x_ref, out_ref.at[me], own_sem)
    own.start()
    pl.semaphore_wait(barrier, count - 1)
    copies = []
    for hop in range(1, count):
        peer = lax.rem(me + hop, count)
        copy = pltpu.make_async_remote_copy(
            src_ref=x_ref.at[peer] if scatter else x_ref,
            dst_ref=out_ref.at[me],
            send_sem=send_sem.at[hop],
            recv_sem=recv_sem.at[hop],
            device_id={axis: peer},
            device_id_type=MESH,
        )
        copy.start()
        copies.append(copy)
    own.wait()
    for copy in copies:
        copy.wait()


def exchange(value, axis, count, scatter, ident):
    shape = value.shape if scatter else (count,) + value.shape
    return pl.pallas_call(
        functools.partial(exchange_kernel, axis, count, scatter),
        out_shape=jax.ShapeDtypeStruct(shape, value.dtype),
        in_specs=[pl.BlockSpec(memory_space=pl.ANY)],
        out_specs=pl.BlockSpec(memory_space=pl.ANY),
        scratch_shapes=[
            pltpu.SemaphoreType.DMA,
            pltpu.SemaphoreType.DMA((count,)),
            pltpu.SemaphoreType.DMA((count,)),
        ],
        compiler_params=pltpu.CompilerParams(collective_id=ident, has_side_effects=True),
    )(value)


def spread_kernel(sends, takes, x_ref, out_ref, own_sem, send_sem, recv_sem):
    me = (lax.axis_index("fsdp"), lax.axis_index("tp"))
    barrier = pltpu.get_barrier_semaphore()

    def other(where):
        return jnp.logical_or(where[0] != me[0], where[1] != me[1])

    for where in takes(me):
        pl.semaphore_signal(barrier, inc=1, device_id=where, device_id_type=MESH)
    targets = sends(me)
    pl.semaphore_wait(barrier, len(targets))

    def remote(index, where, slot):
        return pltpu.make_async_remote_copy(
            src_ref=x_ref,
            dst_ref=out_ref.at[slot],
            send_sem=send_sem.at[index],
            recv_sem=recv_sem.at[slot],
            device_id=where,
            device_id_type=MESH,
        )

    for index, (where, slot) in enumerate(targets):
        @pl.when(other(where))
        def _():
            remote(index, where, slot).start()

        @pl.when(jnp.logical_not(other(where)))
        def _():
            pltpu.make_async_copy(x_ref, out_ref.at[slot], own_sem).start()

    for slot, where in enumerate(takes(me)):
        @pl.when(other(where))
        def _():
            remote(0, where, slot).wait_recv()

        @pl.when(jnp.logical_not(other(where)))
        def _():
            pltpu.make_async_copy(x_ref, out_ref.at[slot], own_sem).wait()

    for index, (where, slot) in enumerate(targets):
        @pl.when(other(where))
        def _():
            remote(index, where, slot).wait_send()


def spread(value, sends, takes, n_sends, n_takes, ident):
    return pl.pallas_call(
        functools.partial(spread_kernel, sends, takes),
        out_shape=jax.ShapeDtypeStruct((n_takes,) + value.shape, value.dtype),
        in_specs=[pl.BlockSpec(memory_space=pl.ANY)],
        out_specs=pl.BlockSpec(memory_space=pl.ANY),
        scratch_shapes=[
            pltpu.SemaphoreType.DMA,
            pltpu.SemaphoreType.DMA((n_sends,)),
            pltpu.SemaphoreType.DMA((n_takes,)),
        ],
        compiler_params=pltpu.CompilerParams(collective_id=ident, has_side_effects=True),
    )(value)


def halves(value):
    head = lax.reduce_precision(value, 8, 7)
    return head.astype(jnp.bfloat16), (value - head).astype(jnp.bfloat16)


def mixed(form, exact, value):
    head, tail = halves(value)
    dot = functools.partial(jnp.einsum, form, preferred_element_type=jnp.float32)
    return dot(exact, head) + dot(exact, tail)


def orthogonal_mix(raw):
    rank = raw.shape[-1]
    eye = jnp.eye(rank, dtype=jnp.float32)
    scale = (jnp.sqrt(jnp.sum(raw * eye, axis=(1, 2))) + NORM_EPS)[:, None, None]
    gram = raw / scale / scale
    mul = functools.partial(jnp.einsum, "mkl,mlj->mkj", precision=HIGH)
    total = None
    for step in range(NS_STEPS):
        mixer = COEF_A * eye + COEF_B * gram + COEF_C * mul(gram, gram)
        total = mixer if total is None else mul(total, mixer)
        if step < NS_STEPS - 1:
            gram = mul(mul(mixer, gram), mixer)
    return total, scale


def body(nf, nt, activations, out_grads, bases, weights, first_moment, second_moment):
    tokens, feats = activations.shape
    mats, rows, rank = bases.shape
    slab = mats * rank // nt
    per = feats // rows
    mine_f, mine_t = lax.axis_index("fsdp"), lax.axis_index("tp")

    def base_sends(me):
        return [
            ((me[1] + nt * i, me[0] // per), lax.rem(me[0], per)) for i in range(nf // nt)
        ]

    def base_takes(me):
        return [(me[1] * per + i, lax.rem(me[0], nt)) for i in range(per)]

    own_bases = spread(bases, base_sends, base_takes, nf // nt, per, 0)
    own_bases = jnp.transpose(own_bases, (0, 2, 1, 3)).reshape(feats, mats * rank)
    outs = exchange(
        jnp.stack([out_grads[j * mats // nt] for j in range(nt)]), "tp", nt, True, 1
    )

    part = mixed("tf,fjk->jtk", activations, own_bases.reshape(feats, nt, slab))
    along = jnp.sum(exchange(part, "tp", nt, True, 2), axis=0)

    part = mixed("jtc,tk->kjc", outs, along).reshape(nf, -1, nt * outs.shape[2])
    part = jnp.sum(exchange(part, "fsdp", nf, True, 3), axis=0)
    proj = exchange(part, "fsdp", nf, False, 4).reshape(slab, nt, -1)

    rank_rows = first_moment.shape[1]
    picked = lax.dynamic_slice_in_dim(proj, lax.rem(mine_f * rank_rows, slab), rank_rows, 0)
    picked = lax.all_gather(picked, "tp")
    picked = lax.dynamic_index_in_dim(picked, mine_t, 2, False)
    spot = mine_f * rank_rows // slab
    own_proj = jnp.stack(
        [lax.dynamic_index_in_dim(picked, m * (nt // mats) + spot, 0, False) for m in range(mats)]
    )
    new_first = BETA_ONE * first_moment + (1.0 - BETA_ONE) * own_proj
    new_second = BETA_TWO * second_moment + (1.0 - BETA_TWO) * own_proj * own_proj
    adam_step = new_first / CORRECT_ONE / (jnp.sqrt(new_second / CORRECT_TWO) + EPSILON)
    step_full = lax.all_gather(adam_step, "fsdp", axis=1, tiled=True)
    new_weights = weights - RATE * jnp.einsum("mdk,mkc->mdc", bases, step_full, precision=HIGH)

    back = mixed("jtc,kjc->tk", outs, proj)
    back = exchange(back, "tp", nt, False, 5)
    part = mixed("tf,jtk->fjk", activations, back).reshape(nf, feats // nf, mats * rank)
    cand = jnp.sum(exchange(part, "fsdp", nf, True, 6), axis=0)

    def cand_sends(me):
        flat = me[1] * nf + me[0]
        return [((flat // nt, i), lax.rem(flat, nt)) for i in range(nt)]

    def cand_takes(me):
        return [
            (lax.rem(me[0] * nt + i, nf), (me[0] * nt) // nf) for i in range(nt)
        ]

    cand = spread(cand, cand_sends, cand_takes, nt, nt, 7).reshape(rows, mats, rank)

    raw = jnp.einsum("dmk,dml->mkl", cand, cand, precision=HIGH)
    raw = jnp.sum(exchange(raw.reshape(nf, -1, rank), "fsdp", nf, True, 8), axis=0)
    raw = exchange(raw, "fsdp", nf, False, 9).reshape(mats, rank, rank)
    mixer, scale = orthogonal_mix(raw)
    new_bases = jnp.einsum("dmk,mkl->mdl", cand, mixer, precision=HIGH) / scale
    return (new_weights, new_first, new_second, new_bases)


def solution(mesh):
    return jax.shard_map(
        functools.partial(body, mesh.shape["fsdp"], mesh.shape["tp"]),
        mesh=mesh,
        in_specs=(
            P("fsdp", "tp"),
            P(None, "fsdp", "tp"),
            P(None, "fsdp", None),
            P(None, "fsdp", "tp"),
            P(None, "fsdp", "tp"),
            P(None, "fsdp", "tp"),
        ),
        out_specs=(
            P(None, "fsdp", "tp"),
            P(None, "fsdp", "tp"),
            P(None, "fsdp", "tp"),
            P(None, "fsdp", None),
        ),
        check_vma=False,
    )
```

```python
import functools

import jax
import jax.numpy as jnp
from jax import lax
from jax.experimental import pallas as pl
from jax.experimental.pallas import tpu as pltpu
from jax.sharding import PartitionSpec as P

NS_STEPS = 5


COEF_A = 3.4445
COEF_B = -4.775
COEF_C = 2.0315
BETA_ONE = 0.9
BETA_TWO = 0.999
CORRECT_ONE = 1.0 - 0.9**10
CORRECT_TWO = 1.0 - 0.999**10
EPSILON = 1e-08
NORM_EPS = 1e-07
RATE = 2.0
HIGH = lax.Precision.HIGHEST
MESH = pl.DeviceIdType.MESH


class Exchange:
    def __init__(self, axis, count, scatter):
        self.axis, self.count, self.scatter = axis, count, scatter

    def shape(self, shape):
        return shape if self.scatter else (self.count,) + shape

    def scratch(self):
        return [
            pltpu.SemaphoreType.DMA,
            pltpu.SemaphoreType.DMA((self.count,)),
            pltpu.SemaphoreType.DMA((self.count,)),
        ]

    def greet(self, barrier):
        me = lax.axis_index(self.axis)
        for hop in range(1, self.count):
            peer = lax.rem(me + hop, self.count)
            pl.semaphore_signal(
                barrier, inc=1, device_id={self.axis: peer}, device_id_type=MESH
            )
        return self.count - 1

    def start(self, x_ref, out_ref, own_sem, send_sem, recv_sem):
        me = lax.axis_index(self.axis)
        own = x_ref.at[me] if self.scatter else x_ref
        self.copies = [pltpu.make_async_copy(own, out_ref.at[me], own_sem)]
        for hop in range(1, self.count):
            peer = lax.rem(me + hop, self.count)
            self.copies.append(
                pltpu.make_async_remote_copy(
                    src_ref=x_ref.at[peer] if self.scatter else x_ref,
                    dst_ref=out_ref.at[me],
                    send_sem=send_sem.at[hop],
                    recv_sem=recv_sem.at[hop],
                    device_id={self.axis: peer},
                    device_id_type=MESH,
                )
            )
        for copy in self.copies[1:]:
            copy.start()
        self.copies[0].start()

    def finish(self, *refs):
        for copy in self.copies:
            copy.wait()


class Spread:
    def __init__(self, sends, takes, n_sends, n_takes):
        self.sends, self.takes, self.n_sends, self.n_takes = sends, takes, n_sends, n_takes

    def shape(self, shape):
        return (self.n_takes,) + shape

    def scratch(self):
        return [
            pltpu.SemaphoreType.DMA,
            pltpu.SemaphoreType.DMA((self.n_sends,)),
            pltpu.SemaphoreType.DMA((self.n_takes,)),
        ]

    def greet(self, barrier):
        for where in self.takes((lax.axis_index("fsdp"), lax.axis_index("tp"))):
            pl.semaphore_signal(barrier, inc=1, device_id=where, device_id_type=MESH)
        return self.n_sends

    def each(self, pairs, remote, local):
        me = (lax.axis_index("fsdp"), lax.axis_index("tp"))
        for index, (where, slot) in enumerate(pairs(me)):
            other = jnp.logical_or(where[0] != me[0], where[1] != me[1])

            @pl.when(other)
            def _():
                remote(index, where, slot)

            if local is not None:

                @pl.when(jnp.logical_not(other))
                def _():
                    local(slot)

    def start(self, x_ref, out_ref, own_sem, send_sem, recv_sem):
        def copy(index, where, slot):
            return pltpu.make_async_remote_copy(
                src_ref=x_ref,
                dst_ref=out_ref.at[slot],
                send_sem=send_sem.at[index],
                recv_sem=recv_sem.at[slot],
                device_id=where,
                device_id_type=MESH,
            )

        self.copy = copy
        self.each(
            self.sends,
            lambda *at: copy(*at).start(),
            lambda slot: pltpu.make_async_copy(x_ref, out_ref.at[slot], own_sem).start(),
        )

    def finish(self, x_ref, out_ref, own_sem, send_sem, recv_sem):
        self.each(
            lambda me: [(where, slot) for slot, where in enumerate(self.takes(me))],
            lambda index, where, slot: self.copy(0, where, slot).wait_recv(),
            lambda slot: pltpu.make_async_copy(x_ref, out_ref.at[slot], own_sem).wait(),
        )
        self.each(self.sends, lambda *at: self.copy(*at).wait_send(), None)


class Chain:
    def __init__(self, count, per, parts):
        self.count, self.per, self.parts = count, per, parts

    def shape(self, shape):
        return shape[:1] + (self.per,) + shape[1:]

    def scratch(self):
        pieces = self.pieces
        return [
            pltpu.SemaphoreType.DMA((pieces,)),
            pltpu.SemaphoreType.DMA((2, pieces)),
            pltpu.SemaphoreType.DMA((pieces,)),
            pltpu.SemaphoreType.DMA((self.per, pieces)),
            pltpu.SemaphoreType.DMA((self.per, pieces)),
        ]

    @property
    def pieces(self):
        return 2 * self.parts

    def places(self):
        me = lax.axis_index("fsdp")
        return me // self.per, lax.rem(me, self.per)

    def mates(self):
        group, spot = self.places()
        return [
            {"fsdp": group * self.per + lax.rem(spot + hop, self.per)}
            for hop in range(1, self.per)
        ]

    def beside(self, step):
        group, spot = self.places()
        return {"fsdp": lax.rem(group + step + self.count, self.count) * self.per + spot}

    def greet(self, barrier):
        for where in self.mates() + [self.beside(1), self.beside(-1)]:
            pl.semaphore_signal(barrier, inc=1, device_id=where, device_id_type=MESH)
        return self.per + 1

    def start(self, x_ref, out_ref, own_sem, pass_sem, come_sem, swap_sem, meet_sem):
        group, spot = self.places()
        source = lax.axis_index("tp")
        size = x_ref.shape[1] // self.parts

        def at(piece, owner):
            mat, part = piece // self.parts, piece % self.parts
            return out_ref.at[mat, owner, pl.ds(part * size, size)]

        def own(piece):
            mat, part = piece // self.parts, piece % self.parts
            return pltpu.make_async_copy(
                x_ref.at[mat, pl.ds(part * size, size)], at(piece, spot), own_sem.at[piece]
            )

        def along(piece, way):
            return pltpu.make_async_remote_copy(
                src_ref=at(piece, spot),
                dst_ref=at(piece, spot),
                send_sem=pass_sem.at[way, piece],
                recv_sem=come_sem.at[piece],
                device_id=self.beside(1 if way == 0 else -1),
                device_id_type=MESH,
            )

        def swap(piece, hop):
            return pltpu.make_async_remote_copy(
                src_ref=at(piece, spot),
                dst_ref=at(piece, spot),
                send_sem=swap_sem.at[hop, piece],
                recv_sem=meet_sem.at[hop, piece],
                device_id=self.mates()[hop - 1],
                device_id_type=MESH,
            )

        onward = (
            jnp.logical_and(group >= source, group < self.count - 1),
            jnp.logical_and(group <= source, group > 0),
        )

        @pl.when(group == source)
        def _():
            for piece in range(self.pieces):
                own(piece).start()

        for piece in range(self.pieces):

            @pl.when(group == source)
            def _():
                own(piece).wait()

            @pl.when(group != source)
            def _():
                along(piece, 0).wait_recv()

            for way in range(2):

                @pl.when(onward[way])
                def _():
                    along(piece, way).start()

            for hop in range(1, self.per):
                swap(piece, hop).start()

        for piece in range(self.pieces):
            for hop in range(1, self.per):
                swap(piece, hop).wait()
            for way in range(2):

                @pl.when(onward[way])
                def _():
                    along(piece, way).wait_send()

    def finish(self, *refs):
        pass


def transfer_kernel(moves, *refs):
    count = len(moves)
    sems, spans = list(refs[2 * count :]), []
    for index, move in enumerate(moves):
        held = len(move.scratch())
        spans.append((refs[index], refs[count + index], *sems[:held]))
        sems = sems[held:]
    barrier = pltpu.get_barrier_semaphore()
    pl.semaphore_wait(barrier, sum(move.greet(barrier) for move in moves))
    for move, span in zip(moves, spans):
        move.start(*span)
    for move, span in zip(moves, spans):
        move.finish(*span)


def transfer(ident, *pairs):
    values, moves = [pair[0] for pair in pairs], [pair[1] for pair in pairs]
    results = pl.pallas_call(
        functools.partial(transfer_kernel, moves),
        out_shape=[
            jax.ShapeDtypeStruct(move.shape(value.shape), value.dtype)
            for value, move in zip(values, moves)
        ],
        in_specs=[pl.BlockSpec(memory_space=pl.ANY)] * len(values),
        out_specs=[pl.BlockSpec(memory_space=pl.ANY)] * len(values),
        scratch_shapes=[sem for move in moves for sem in move.scratch()],
        compiler_params=pltpu.CompilerParams(collective_id=ident, has_side_effects=True),
    )(*values)
    return results[0] if len(results) == 1 else results


def halves(value):
    head = lax.reduce_precision(value, 8, 7)
    return head.astype(jnp.bfloat16), (value - head).astype(jnp.bfloat16)


def mixed(form, exact, value):
    head, tail = halves(value)
    dot = functools.partial(jnp.einsum, form, preferred_element_type=jnp.float32)
    return dot(exact, head) + dot(exact, tail)


def orthogonal_mix(raw):
    rank = raw.shape[-1]
    eye = jnp.eye(rank, dtype=jnp.float32)
    scale = (jnp.sqrt(jnp.sum(raw * eye, axis=(1, 2))) + NORM_EPS)[:, None, None]
    gram = raw / scale / scale
    mul = functools.partial(jnp.einsum, "mkl,mlj->mkj", precision=HIGH)
    total = None
    for step in range(NS_STEPS):
        mixer = COEF_A * eye + COEF_B * gram + COEF_C * mul(gram, gram)
        total = mixer if total is None else mul(total, mixer)
        if step < NS_STEPS - 1:
            gram = mul(mul(mixer, gram), mixer)
    return total, scale


def body(nf, nt, activations, out_grads, bases, weights, first_moment, second_moment):
    tokens, feats = activations.shape
    mats, rows, rank = bases.shape
    slab = mats * rank // nt
    per = feats // rows
    mine_f, mine_t = lax.axis_index("fsdp"), lax.axis_index("tp")

    outs, own_bases = transfer(
        0,
        (jnp.stack([out_grads[j * mats // nt] for j in range(nt)]), Exchange("tp", nt, True)),
        (bases, Chain(nf // per, per, 2)),
    )
    own_bases = own_bases.reshape(mats, feats, rank)

    part = mixed("tf,mfk->mtk", activations, own_bases)
    part = part.reshape(mats, tokens, nt // mats, slab)
    part = jnp.transpose(part, (0, 2, 1, 3)).reshape(nt, tokens, slab)
    along = jnp.sum(transfer(1, (part, Exchange("tp", nt, True))), axis=0)

    part = mixed("jtc,tk->kjc", outs, along).reshape(nf, -1, nt * outs.shape[2])
    part = jnp.sum(transfer(2, (part, Exchange("fsdp", nf, True))), axis=0)
    proj = transfer(3, (part, Exchange("fsdp", nf, False))).reshape(slab, nt, -1)

    rank_rows = first_moment.shape[1]
    picked = lax.dynamic_slice_in_dim(proj, lax.rem(mine_f * rank_rows, slab), rank_rows, 0)
    back = mixed("jtc,kjc->tk", outs, proj)
    back, picked = transfer(
        4,
        (back, Exchange("tp", nt, False)),
        (jnp.transpose(picked, (1, 0, 2)), Exchange("tp", nt, True)),
    )

    spot = mine_f * rank_rows // slab
    own_proj = jnp.stack(
        [lax.dynamic_index_in_dim(picked, m * (nt // mats) + spot, 0, False) for m in range(mats)]
    )
    new_first = BETA_ONE * first_moment + (1.0 - BETA_ONE) * own_proj
    new_second = BETA_TWO * second_moment + (1.0 - BETA_TWO) * own_proj * own_proj
    adam_step = new_first / CORRECT_ONE / (jnp.sqrt(new_second / CORRECT_TWO) + EPSILON)

    part = mixed("tf,jtk->fjk", activations, back).reshape(nf, feats // nf, mats * rank)
    cand, step_full = transfer(
        5,
        (part, Exchange("fsdp", nf, True)),
        (adam_step, Exchange("fsdp", nf, False)),
    )
    cand = jnp.sum(cand, axis=0)
    step_full = jnp.transpose(step_full, (1, 0, 2, 3)).reshape(mats, rank, -1)
    new_weights = weights - RATE * jnp.einsum("mdk,mkc->mdc", bases, step_full, precision=HIGH)

    def cand_sends(me):
        flat = me[1] * nf + me[0]
        return [((flat // nt, i), lax.rem(flat, nt)) for i in range(nt)]

    def cand_takes(me):
        return [
            (lax.rem(me[0] * nt + i, nf), (me[0] * nt) // nf) for i in range(nt)
        ]

    raw = cand.reshape(-1, mats, rank)
    raw = jnp.einsum("dmk,dml->mkl", raw, raw, precision=HIGH).reshape(nf, -1, rank)
    raw, cand = transfer(
        6,
        (raw, Exchange("fsdp", nf, True)),
        (cand, Spread(cand_sends, cand_takes, nt, nt)),
    )
    cand = cand.reshape(rows, mats, rank)
    raw = jnp.sum(raw, axis=0)
    raw = jnp.sum(transfer(7, (raw, Exchange("tp", nt, False))), axis=0)
    raw = transfer(8, (raw, Exchange("fsdp", nf, False))).reshape(mats, rank, rank)
    mixer, scale = orthogonal_mix(raw)
    new_bases = jnp.einsum("dmk,mkl->mdl", cand, mixer, precision=HIGH) / scale
    return (new_weights, new_first, new_second, new_bases)


def solution(mesh):
    return jax.shard_map(
        functools.partial(body, mesh.shape["fsdp"], mesh.shape["tp"]),
        mesh=mesh,
        in_specs=(
            P("fsdp", "tp"),
            P(None, "fsdp", "tp"),
            P(None, "fsdp", None),
            P(None, "fsdp", "tp"),
            P(None, "fsdp", "tp"),
            P(None, "fsdp", "tp"),
        ),
        out_specs=(
            P(None, "fsdp", "tp"),
            P(None, "fsdp", "tp"),
            P(None, "fsdp", "tp"),
            P(None, "fsdp", None),
        ),
        check_vma=False,
    )
```

```python
import functools

import jax
import jax.numpy as jnp
from jax import lax
from jax.experimental import pallas as pl
from jax.experimental.pallas import tpu as pltpu
from jax.sharding import PartitionSpec as P

NS_STEPS = 5


COEF_A = 3.4445
COEF_B = -4.775
COEF_C = 2.0315
BETA_ONE = 0.9
BETA_TWO = 0.999
CORRECT_ONE = 1.0 - 0.9**10
CORRECT_TWO = 1.0 - 0.999**10
EPSILON = 1e-08
NORM_EPS = 1e-07
RATE = 2.0
HIGH = lax.Precision.HIGHEST
MESH = pl.DeviceIdType.MESH


class Exchange:
    def __init__(self, axis, count, scatter):
        self.axis, self.count, self.scatter = axis, count, scatter

    def shape(self, shape):
        return shape if self.scatter else (self.count,) + shape

    def scratch(self):
        return [
            pltpu.SemaphoreType.DMA,
            pltpu.SemaphoreType.DMA((self.count,)),
            pltpu.SemaphoreType.DMA((self.count,)),
        ]

    def greet(self, barrier):
        me = lax.axis_index(self.axis)
        for hop in range(1, self.count):
            peer = lax.rem(me + hop, self.count)
            pl.semaphore_signal(
                barrier, inc=1, device_id={self.axis: peer}, device_id_type=MESH
            )
        return self.count - 1

    def start(self, x_ref, out_ref, own_sem, send_sem, recv_sem):
        me = lax.axis_index(self.axis)
        own = x_ref.at[me] if self.scatter else x_ref
        self.copies = [pltpu.make_async_copy(own, out_ref.at[me], own_sem)]
        for hop in range(1, self.count):
            peer = lax.rem(me + hop, self.count)
            self.copies.append(
                pltpu.make_async_remote_copy(
                    src_ref=x_ref.at[peer] if self.scatter else x_ref,
                    dst_ref=out_ref.at[me],
                    send_sem=send_sem.at[hop],
                    recv_sem=recv_sem.at[hop],
                    device_id={self.axis: peer},
                    device_id_type=MESH,
                )
            )
        for copy in self.copies[1:]:
            copy.start()
        self.copies[0].start()

    def finish(self, *refs):
        for copy in self.copies:
            copy.wait()


class Spread:
    def __init__(self, sends, takes, n_sends, n_takes):
        self.sends, self.takes, self.n_sends, self.n_takes = sends, takes, n_sends, n_takes

    def shape(self, shape):
        return (self.n_takes,) + shape

    def scratch(self):
        return [
            pltpu.SemaphoreType.DMA,
            pltpu.SemaphoreType.DMA((self.n_sends,)),
            pltpu.SemaphoreType.DMA((self.n_takes,)),
        ]

    def greet(self, barrier):
        for where in self.takes((lax.axis_index("fsdp"), lax.axis_index("tp"))):
            pl.semaphore_signal(barrier, inc=1, device_id=where, device_id_type=MESH)
        return self.n_sends

    def each(self, pairs, remote, local):
        me = (lax.axis_index("fsdp"), lax.axis_index("tp"))
        for index, (where, slot) in enumerate(pairs(me)):
            other = jnp.logical_or(where[0] != me[0], where[1] != me[1])

            @pl.when(other)
            def _():
                remote(index, where, slot)

            if local is not None:

                @pl.when(jnp.logical_not(other))
                def _():
                    local(slot)

    def start(self, x_ref, out_ref, own_sem, send_sem, recv_sem):
        def copy(index, where, slot):
            return pltpu.make_async_remote_copy(
                src_ref=x_ref,
                dst_ref=out_ref.at[slot],
                send_sem=send_sem.at[index],
                recv_sem=recv_sem.at[slot],
                device_id=where,
                device_id_type=MESH,
            )

        self.copy = copy
        self.each(
            self.sends,
            lambda *at: copy(*at).start(),
            lambda slot: pltpu.make_async_copy(x_ref, out_ref.at[slot], own_sem).start(),
        )

    def finish(self, x_ref, out_ref, own_sem, send_sem, recv_sem):
        self.each(
            lambda me: [(where, slot) for slot, where in enumerate(self.takes(me))],
            lambda index, where, slot: self.copy(0, where, slot).wait_recv(),
            lambda slot: pltpu.make_async_copy(x_ref, out_ref.at[slot], own_sem).wait(),
        )
        self.each(self.sends, lambda *at: self.copy(*at).wait_send(), None)


class Chain:
    def __init__(self, count, per, parts):
        self.count, self.per, self.parts = count, per, parts

    def shape(self, shape):
        return shape[:1] + (self.per,) + shape[1:]

    def scratch(self):
        pieces = self.pieces
        return [
            pltpu.SemaphoreType.DMA((pieces,)),
            pltpu.SemaphoreType.DMA((2, pieces)),
            pltpu.SemaphoreType.DMA((pieces,)),
            pltpu.SemaphoreType.DMA((self.per, pieces)),
            pltpu.SemaphoreType.DMA((self.per, pieces)),
        ]

    @property
    def pieces(self):
        return 2 * self.parts

    def places(self):
        me = lax.axis_index("fsdp")
        return me // self.per, lax.rem(me, self.per)

    def mates(self):
        group, spot = self.places()
        return [
            {"fsdp": group * self.per + lax.rem(spot + hop, self.per)}
            for hop in range(1, self.per)
        ]

    def beside(self, step):
        group, spot = self.places()
        return {"fsdp": lax.rem(group + step + self.count, self.count) * self.per + spot}

    def greet(self, barrier):
        for where in self.mates() + [self.beside(1), self.beside(-1)]:
            pl.semaphore_signal(barrier, inc=1, device_id=where, device_id_type=MESH)
        return self.per + 1

    def start(self, x_ref, out_ref, own_sem, pass_sem, come_sem, swap_sem, meet_sem):
        group, spot = self.places()
        source = lax.axis_index("tp")
        size = x_ref.shape[1] // self.parts

        def at(piece, owner):
            mat, part = piece // self.parts, piece % self.parts
            return out_ref.at[mat, owner, pl.ds(part * size, size)]

        def own(piece):
            mat, part = piece // self.parts, piece % self.parts
            return pltpu.make_async_copy(
                x_ref.at[mat, pl.ds(part * size, size)], at(piece, spot), own_sem.at[piece]
            )

        def along(piece, way):
            return pltpu.make_async_remote_copy(
                src_ref=at(piece, spot),
                dst_ref=at(piece, spot),
                send_sem=pass_sem.at[way, piece],
                recv_sem=come_sem.at[piece],
                device_id=self.beside(1 if way == 0 else -1),
                device_id_type=MESH,
            )

        def swap(piece, hop):
            return pltpu.make_async_remote_copy(
                src_ref=at(piece, spot),
                dst_ref=at(piece, spot),
                send_sem=swap_sem.at[hop, piece],
                recv_sem=meet_sem.at[hop, piece],
                device_id=self.mates()[hop - 1],
                device_id_type=MESH,
            )

        onward = (
            jnp.logical_and(group >= source, group < self.count - 1),
            jnp.logical_and(group <= source, group > 0),
        )

        @pl.when(group == source)
        def _():
            for piece in range(self.pieces):
                own(piece).start()

        for piece in range(self.pieces):

            @pl.when(group == source)
            def _():
                own(piece).wait()

            @pl.when(group != source)
            def _():
                along(piece, 0).wait_recv()

            for way in range(2):

                @pl.when(onward[way])
                def _():
                    along(piece, way).start()

            for hop in range(1, self.per):
                swap(piece, hop).start()

        for piece in range(self.pieces):
            for hop in range(1, self.per):
                swap(piece, hop).wait()
            for way in range(2):

                @pl.when(onward[way])
                def _():
                    along(piece, way).wait_send()

    def finish(self, *refs):
        pass


def transfer_kernel(moves, *refs):
    count = len(moves)
    sems, spans = list(refs[2 * count :]), []
    for index, move in enumerate(moves):
        held = len(move.scratch())
        spans.append((refs[index], refs[count + index], *sems[:held]))
        sems = sems[held:]
    barrier = pltpu.get_barrier_semaphore()
    pl.semaphore_wait(barrier, sum(move.greet(barrier) for move in moves))
    for move, span in zip(moves, spans):
        move.start(*span)
    for move, span in zip(moves, spans):
        move.finish(*span)


def transfer(ident, *pairs):
    values, moves = [pair[0] for pair in pairs], [pair[1] for pair in pairs]
    results = pl.pallas_call(
        functools.partial(transfer_kernel, moves),
        out_shape=[
            jax.ShapeDtypeStruct(move.shape(value.shape), value.dtype)
            for value, move in zip(values, moves)
        ],
        in_specs=[pl.BlockSpec(memory_space=pl.ANY)] * len(values),
        out_specs=[pl.BlockSpec(memory_space=pl.ANY)] * len(values),
        scratch_shapes=[sem for move in moves for sem in move.scratch()],
        compiler_params=pltpu.CompilerParams(collective_id=ident, has_side_effects=True),
    )(*values)
    return results[0] if len(results) == 1 else results


def halves(value):
    head = lax.reduce_precision(value, 8, 7)
    return head.astype(jnp.bfloat16), (value - head).astype(jnp.bfloat16)


def mixed(form, exact, value):
    head, tail = halves(value)
    dot = functools.partial(jnp.einsum, form, preferred_element_type=jnp.float32)
    return dot(exact, head) + dot(exact, tail)


def orthogonal_mix(raw):
    rank = raw.shape[-1]
    eye = jnp.eye(rank, dtype=jnp.float32)
    scale = (jnp.sqrt(jnp.sum(raw * eye, axis=(1, 2))) + NORM_EPS)[:, None, None]
    gram = raw / scale / scale
    mul = functools.partial(jnp.einsum, "mkl,mlj->mkj", precision=HIGH)
    total = None
    for step in range(NS_STEPS):
        mixer = COEF_A * eye + COEF_B * gram + COEF_C * mul(gram, gram)
        total = mixer if total is None else mul(total, mixer)
        if step < NS_STEPS - 1:
            gram = mul(mul(mixer, gram), mixer)
    return total, scale


def body(nf, nt, activations, out_grads, bases, weights, first_moment, second_moment):
    tokens, feats = activations.shape
    mats, rows, rank = bases.shape
    slab = mats * rank // nt
    per = feats // rows
    mine_f, mine_t = lax.axis_index("fsdp"), lax.axis_index("tp")

    outs, own_bases = transfer(
        0,
        (jnp.stack([out_grads[j * mats // nt] for j in range(nt)]), Exchange("tp", nt, True)),
        (bases, Chain(nf // per, per, 8)),
    )
    own_bases = own_bases.reshape(mats, feats, rank)

    part = mixed("tf,mfk->mtk", activations, own_bases)
    part = part.reshape(mats, tokens, nt // mats, slab)
    part = jnp.transpose(part, (0, 2, 1, 3)).reshape(nt, tokens, slab)
    along = jnp.sum(transfer(1, (part, Exchange("tp", nt, True))), axis=0)

    part = mixed("jtc,tk->kjc", outs, along).reshape(nf, -1, nt * outs.shape[2])
    part = jnp.sum(transfer(2, (part, Exchange("fsdp", nf, True))), axis=0)
    proj = transfer(3, (part, Exchange("fsdp", nf, False))).reshape(slab, nt, -1)

    rank_rows = first_moment.shape[1]
    picked = lax.dynamic_slice_in_dim(proj, lax.rem(mine_f * rank_rows, slab), rank_rows, 0)
    back = mixed("jtc,kjc->tk", outs, proj)
    back, picked = transfer(
        4,
        (back, Exchange("tp", nt, False)),
        (jnp.transpose(picked, (1, 0, 2)), Exchange("tp", nt, True)),
    )

    spot = mine_f * rank_rows // slab
    own_proj = jnp.stack(
        [lax.dynamic_index_in_dim(picked, m * (nt // mats) + spot, 0, False) for m in range(mats)]
    )
    new_first = BETA_ONE * first_moment + (1.0 - BETA_ONE) * own_proj
    new_second = BETA_TWO * second_moment + (1.0 - BETA_TWO) * own_proj * own_proj
    adam_step = new_first / CORRECT_ONE / (jnp.sqrt(new_second / CORRECT_TWO) + EPSILON)

    part = mixed("tf,jtk->fjk", activations, back).reshape(nf, feats // nf, mats * rank)
    cand, step_full = transfer(
        5,
        (part, Exchange("fsdp", nf, True)),
        (adam_step, Exchange("fsdp", nf, False)),
    )
    cand = jnp.sum(cand, axis=0)
    step_full = jnp.transpose(step_full, (1, 0, 2, 3)).reshape(mats, rank, -1)
    new_weights = weights - RATE * jnp.einsum("mdk,mkc->mdc", bases, step_full, precision=HIGH)

    def cand_sends(me):
        flat = me[1] * nf + me[0]
        return [((flat // nt, lax.rem(flat, nt)), 0)]

    def cand_takes(me):
        flat = me[0] * nt + me[1]
        return [(lax.rem(flat, nf), flat // nf)]

    raw = cand.reshape(-1, mats, rank)
    raw = jnp.einsum("dmk,dml->mkl", raw, raw, precision=HIGH).reshape(nf, -1, rank)
    raw, cand = transfer(
        6,
        (raw, Exchange("fsdp", nf, True)),
        (cand, Spread(cand_sends, cand_takes, 1, 1)),
    )
    raw = jnp.sum(raw, axis=0)
    raw, cand = transfer(
        7, (raw, Exchange("tp", nt, False)), (cand[0], Exchange("tp", nt, False))
    )
    cand = cand.reshape(rows, mats, rank)
    raw = jnp.sum(raw, axis=0)
    raw = transfer(8, (raw, Exchange("fsdp", nf, False))).reshape(mats, rank, rank)
    mixer, scale = orthogonal_mix(raw)
    new_bases = jnp.einsum("dmk,mkl->mdl", cand, mixer, precision=HIGH) / scale
    return (new_weights, new_first, new_second, new_bases)


def solution(mesh):
    return jax.shard_map(
        functools.partial(body, mesh.shape["fsdp"], mesh.shape["tp"]),
        mesh=mesh,
        in_specs=(
            P("fsdp", "tp"),
            P(None, "fsdp", "tp"),
            P(None, "fsdp", None),
            P(None, "fsdp", "tp"),
            P(None, "fsdp", "tp"),
            P(None, "fsdp", "tp"),
        ),
        out_specs=(
            P(None, "fsdp", "tp"),
            P(None, "fsdp", "tp"),
            P(None, "fsdp", "tp"),
            P(None, "fsdp", None),
        ),
        check_vma=False,
    )
```

```python
import functools

import jax
import jax.numpy as jnp
from jax import lax
from jax.experimental import pallas as pl
from jax.experimental.pallas import tpu as pltpu
from jax.sharding import PartitionSpec as P

NS_STEPS = 5


COEF_A = 3.4445
COEF_B = -4.775
COEF_C = 2.0315
BETA_ONE = 0.9
BETA_TWO = 0.999
CORRECT_ONE = 1.0 - 0.9**10
CORRECT_TWO = 1.0 - 0.999**10
EPSILON = 1e-08
NORM_EPS = 1e-07
RATE = 2.0
HIGH = lax.Precision.HIGHEST
MESH = pl.DeviceIdType.MESH


class Exchange:
    def __init__(self, axis, count, scatter, stride=1):
        self.axis, self.count, self.scatter, self.stride = axis, count, scatter, stride

    def place(self):
        return lax.rem(lax.axis_index(self.axis) // self.stride, self.count)

    def where(self, peer):
        index = lax.axis_index(self.axis)
        return {self.axis: index + (peer - self.place()) * self.stride}

    def shape(self, shape):
        return shape if self.scatter else (self.count,) + shape

    def scratch(self):
        return [
            pltpu.SemaphoreType.DMA,
            pltpu.SemaphoreType.DMA((self.count,)),
            pltpu.SemaphoreType.DMA((self.count,)),
        ]

    def greet(self, barrier):
        me = self.place()
        for hop in range(1, self.count):
            peer = lax.rem(me + hop, self.count)
            pl.semaphore_signal(
                barrier, inc=1, device_id=self.where(peer), device_id_type=MESH
            )
        return self.count - 1

    def start(self, x_ref, out_ref, own_sem, send_sem, recv_sem):
        me = self.place()
        own = x_ref.at[me] if self.scatter else x_ref
        self.copies = [pltpu.make_async_copy(own, out_ref.at[me], own_sem)]
        for hop in range(1, self.count):
            peer = lax.rem(me + hop, self.count)
            self.copies.append(
                pltpu.make_async_remote_copy(
                    src_ref=x_ref.at[peer] if self.scatter else x_ref,
                    dst_ref=out_ref.at[me],
                    send_sem=send_sem.at[hop],
                    recv_sem=recv_sem.at[hop],
                    device_id=self.where(peer),
                    device_id_type=MESH,
                )
            )
        for copy in self.copies[1:]:
            copy.start()
        self.copies[0].start()

    def finish(self, *refs):
        for copy in self.copies:
            copy.wait()


class Spread:
    def __init__(self, sends, takes, n_sends, n_takes):
        self.sends, self.takes, self.n_sends, self.n_takes = sends, takes, n_sends, n_takes

    def shape(self, shape):
        return (self.n_takes,) + shape

    def scratch(self):
        return [
            pltpu.SemaphoreType.DMA,
            pltpu.SemaphoreType.DMA((self.n_sends,)),
            pltpu.SemaphoreType.DMA((self.n_takes,)),
        ]

    def greet(self, barrier):
        for where in self.takes((lax.axis_index("fsdp"), lax.axis_index("tp"))):
            pl.semaphore_signal(barrier, inc=1, device_id=where, device_id_type=MESH)
        return self.n_sends

    def each(self, pairs, remote, local):
        me = (lax.axis_index("fsdp"), lax.axis_index("tp"))
        for index, (where, slot) in enumerate(pairs(me)):
            other = jnp.logical_or(where[0] != me[0], where[1] != me[1])

            @pl.when(other)
            def _():
                remote(index, where, slot)

            if local is not None:

                @pl.when(jnp.logical_not(other))
                def _():
                    local(slot)

    def start(self, x_ref, out_ref, own_sem, send_sem, recv_sem):
        def copy(index, where, slot):
            return pltpu.make_async_remote_copy(
                src_ref=x_ref,
                dst_ref=out_ref.at[slot],
                send_sem=send_sem.at[index],
                recv_sem=recv_sem.at[slot],
                device_id=where,
                device_id_type=MESH,
            )

        self.copy = copy
        self.each(
            self.sends,
            lambda *at: copy(*at).start(),
            lambda slot: pltpu.make_async_copy(x_ref, out_ref.at[slot], own_sem).start(),
        )

    def finish(self, x_ref, out_ref, own_sem, send_sem, recv_sem):
        self.each(
            lambda me: [(where, slot) for slot, where in enumerate(self.takes(me))],
            lambda index, where, slot: self.copy(0, where, slot).wait_recv(),
            lambda slot: pltpu.make_async_copy(x_ref, out_ref.at[slot], own_sem).wait(),
        )
        self.each(self.sends, lambda *at: self.copy(*at).wait_send(), None)


class Chain:
    def __init__(self, count, per, parts):
        self.count, self.per, self.parts = count, per, parts

    def shape(self, shape):
        return shape[:1] + (self.per,) + shape[1:]

    def scratch(self):
        pieces = self.pieces
        return [
            pltpu.SemaphoreType.DMA((pieces,)),
            pltpu.SemaphoreType.DMA((2, pieces)),
            pltpu.SemaphoreType.DMA((pieces,)),
            pltpu.SemaphoreType.DMA((self.per, pieces)),
            pltpu.SemaphoreType.DMA((self.per, pieces)),
        ]

    @property
    def pieces(self):
        return 2 * self.parts

    def places(self):
        me = lax.axis_index("fsdp")
        return me // self.per, lax.rem(me, self.per)

    def mates(self):
        group, spot = self.places()
        return [
            {"fsdp": group * self.per + lax.rem(spot + hop, self.per)}
            for hop in range(1, self.per)
        ]

    def beside(self, step):
        group, spot = self.places()
        return {"fsdp": lax.rem(group + step + self.count, self.count) * self.per + spot}

    def greet(self, barrier):
        for where in self.mates() + [self.beside(1), self.beside(-1)]:
            pl.semaphore_signal(barrier, inc=1, device_id=where, device_id_type=MESH)
        return self.per + 1

    def start(self, x_ref, out_ref, own_sem, pass_sem, come_sem, swap_sem, meet_sem):
        group, spot = self.places()
        source = lax.axis_index("tp")
        size = x_ref.shape[1] // self.parts

        def at(piece, owner):
            mat, part = piece // self.parts, piece % self.parts
            return out_ref.at[mat, owner, pl.ds(part * size, size)]

        def own(piece):
            mat, part = piece // self.parts, piece % self.parts
            return pltpu.make_async_copy(
                x_ref.at[mat, pl.ds(part * size, size)], at(piece, spot), own_sem.at[piece]
            )

        def along(piece, way):
            return pltpu.make_async_remote_copy(
                src_ref=at(piece, spot),
                dst_ref=at(piece, spot),
                send_sem=pass_sem.at[way, piece],
                recv_sem=come_sem.at[piece],
                device_id=self.beside(1 if way == 0 else -1),
                device_id_type=MESH,
            )

        def swap(piece, hop):
            return pltpu.make_async_remote_copy(
                src_ref=at(piece, spot),
                dst_ref=at(piece, spot),
                send_sem=swap_sem.at[hop, piece],
                recv_sem=meet_sem.at[hop, piece],
                device_id=self.mates()[hop - 1],
                device_id_type=MESH,
            )

        onward = (
            jnp.logical_and(group >= source, group < self.count - 1),
            jnp.logical_and(group <= source, group > 0),
        )

        @pl.when(group == source)
        def _():
            for piece in range(self.pieces):
                own(piece).start()

        for piece in range(self.pieces):

            @pl.when(group == source)
            def _():
                own(piece).wait()

            @pl.when(group != source)
            def _():
                along(piece, 0).wait_recv()

            for way in range(2):

                @pl.when(onward[way])
                def _():
                    along(piece, way).start()

            for hop in range(1, self.per):
                swap(piece, hop).start()

        for piece in range(self.pieces):
            for hop in range(1, self.per):
                swap(piece, hop).wait()
            for way in range(2):

                @pl.when(onward[way])
                def _():
                    along(piece, way).wait_send()

    def finish(self, *refs):
        pass


def transfer_kernel(moves, *refs):
    count = len(moves)
    sems, spans = list(refs[2 * count :]), []
    for index, move in enumerate(moves):
        held = len(move.scratch())
        spans.append((refs[index], refs[count + index], *sems[:held]))
        sems = sems[held:]
    barrier = pltpu.get_barrier_semaphore()
    pl.semaphore_wait(barrier, sum(move.greet(barrier) for move in moves))
    for move, span in zip(moves, spans):
        move.start(*span)
    for move, span in zip(moves, spans):
        move.finish(*span)


def transfer(ident, *pairs):
    values, moves = [pair[0] for pair in pairs], [pair[1] for pair in pairs]
    results = pl.pallas_call(
        functools.partial(transfer_kernel, moves),
        out_shape=[
            jax.ShapeDtypeStruct(move.shape(value.shape), value.dtype)
            for value, move in zip(values, moves)
        ],
        in_specs=[pl.BlockSpec(memory_space=pl.ANY)] * len(values),
        out_specs=[pl.BlockSpec(memory_space=pl.ANY)] * len(values),
        scratch_shapes=[sem for move in moves for sem in move.scratch()],
        compiler_params=pltpu.CompilerParams(collective_id=ident, has_side_effects=True),
    )(*values)
    return results[0] if len(results) == 1 else results


def halves(value):
    head = lax.reduce_precision(value, 8, 7)
    return head.astype(jnp.bfloat16), (value - head).astype(jnp.bfloat16)


def mixed(form, exact, value):
    head, tail = halves(value)
    dot = functools.partial(jnp.einsum, form, preferred_element_type=jnp.float32)
    return dot(exact, head) + dot(exact, tail)


def orthogonal_mix(raw):
    rank = raw.shape[-1]
    eye = jnp.eye(rank, dtype=jnp.float32)
    scale = (jnp.sqrt(jnp.sum(raw * eye, axis=(1, 2))) + NORM_EPS)[:, None, None]
    gram = raw / scale / scale
    mul = functools.partial(jnp.einsum, "mkl,mlj->mkj", precision=HIGH)
    total = None
    for step in range(NS_STEPS):
        mixer = COEF_A * eye + COEF_B * gram + COEF_C * mul(gram, gram)
        total = mixer if total is None else mul(total, mixer)
        if step < NS_STEPS - 1:
            gram = mul(mul(mixer, gram), mixer)
    return total, scale


def body(nf, nt, activations, out_grads, bases, weights, first_moment, second_moment):
    tokens, feats = activations.shape
    mats, rows, rank = bases.shape
    slab = mats * rank // nt
    per = feats // rows
    mine_f, mine_t = lax.axis_index("fsdp"), lax.axis_index("tp")

    outs, own_bases = transfer(
        0,
        (jnp.stack([out_grads[j * mats // nt] for j in range(nt)]), Exchange("tp", nt, True)),
        (bases, Chain(nf // per, per, 8)),
    )
    own_bases = own_bases.reshape(mats, feats, rank)

    part = mixed("tf,mfk->mtk", activations, own_bases)
    part = part.reshape(mats, tokens, nt // mats, slab)
    part = jnp.transpose(part, (0, 2, 1, 3)).reshape(nt, tokens, slab)
    along = jnp.sum(transfer(1, (part, Exchange("tp", nt, True))), axis=0)

    part = mixed("jtc,tk->kjc", outs, along).reshape(nf, -1, nt * outs.shape[2])
    part = jnp.sum(transfer(2, (part, Exchange("fsdp", nf, True))), axis=0)
    proj = transfer(3, (part, Exchange("fsdp", nf, False))).reshape(slab, nt, -1)

    rank_rows = first_moment.shape[1]
    picked = lax.dynamic_slice_in_dim(proj, lax.rem(mine_f * rank_rows, slab), rank_rows, 0)
    back = mixed("jtc,kjc->tk", outs, proj)
    back, picked = transfer(
        4,
        (back, Exchange("tp", nt, False)),
        (jnp.transpose(picked, (1, 0, 2)), Exchange("tp", nt, True)),
    )

    spot = mine_f * rank_rows // slab
    own_proj = jnp.stack(
        [lax.dynamic_index_in_dim(picked, m * (nt // mats) + spot, 0, False) for m in range(mats)]
    )
    new_first = BETA_ONE * first_moment + (1.0 - BETA_ONE) * own_proj
    new_second = BETA_TWO * second_moment + (1.0 - BETA_TWO) * own_proj * own_proj
    adam_step = new_first / CORRECT_ONE / (jnp.sqrt(new_second / CORRECT_TWO) + EPSILON)

    groups = nf // per
    part = mixed("tf,jtk->fjk", activations, back).reshape(groups, per, -1, mats * rank)
    upper = part.shape[2] * 11 // 16 // 8 * 8
    near, far = transfer(
        5,
        (jnp.swapaxes(part[:, :, :upper], 0, 1), Exchange("fsdp", per, True)),
        (part[:, :, upper:], Exchange("fsdp", groups, True, per)),
    )
    near, far = transfer(
        9,
        (jnp.sum(near, axis=0), Exchange("fsdp", groups, True, per)),
        (jnp.sum(far, axis=0), Exchange("fsdp", per, True)),
    )
    cand = jnp.concatenate([jnp.sum(near, axis=0), jnp.sum(far, axis=0)])

    def cand_sends(me):
        flat = me[1] * nf + me[0]
        return [((flat // nt, lax.rem(flat, nt)), 0)]

    def cand_takes(me):
        flat = me[0] * nt + me[1]
        return [(lax.rem(flat, nf), flat // nf)]

    raw = cand.reshape(-1, mats, rank)
    raw = jnp.einsum("dmk,dml->mkl", raw, raw, precision=HIGH).reshape(nf, -1, rank)
    raw, cand = transfer(
        6,
        (raw, Exchange("fsdp", nf, True)),
        (cand, Spread(cand_sends, cand_takes, 1, 1)),
    )
    raw = jnp.sum(raw, axis=0)
    raw, cand, step_full = transfer(
        7,
        (raw, Exchange("tp", nt, False)),
        (cand[0], Exchange("tp", nt, False)),
        (adam_step, Exchange("fsdp", nf, False)),
    )
    step_full = jnp.transpose(step_full, (1, 0, 2, 3)).reshape(mats, rank, -1)
    new_weights = weights - RATE * jnp.einsum("mdk,mkc->mdc", bases, step_full, precision=HIGH)
    cand = cand.reshape(rows, mats, rank)
    raw = jnp.sum(raw, axis=0)
    raw = transfer(8, (raw, Exchange("fsdp", nf, False))).reshape(mats, rank, rank)
    mixer, scale = orthogonal_mix(raw)
    new_bases = jnp.einsum("dmk,mkl->mdl", cand, mixer, precision=HIGH) / scale
    return (new_weights, new_first, new_second, new_bases)


def solution(mesh):
    return jax.shard_map(
        functools.partial(body, mesh.shape["fsdp"], mesh.shape["tp"]),
        mesh=mesh,
        in_specs=(
            P("fsdp", "tp"),
            P(None, "fsdp", "tp"),
            P(None, "fsdp", None),
            P(None, "fsdp", "tp"),
            P(None, "fsdp", "tp"),
            P(None, "fsdp", "tp"),
        ),
        out_specs=(
            P(None, "fsdp", "tp"),
            P(None, "fsdp", "tp"),
            P(None, "fsdp", "tp"),
            P(None, "fsdp", None),
        ),
        check_vma=False,
    )
```

```python
import functools

import jax
import jax.numpy as jnp
from jax import lax
from jax.experimental import pallas as pl
from jax.experimental.pallas import tpu as pltpu
from jax.sharding import PartitionSpec as P

NS_STEPS = 5


COEF_A = 3.4445
COEF_B = -4.775
COEF_C = 2.0315
BETA_ONE = 0.9
BETA_TWO = 0.999
CORRECT_ONE = 1.0 - 0.9**10
CORRECT_TWO = 1.0 - 0.999**10
EPSILON = 1e-08
NORM_EPS = 1e-07
RATE = 2.0
HIGH = lax.Precision.HIGHEST
MESH = pl.DeviceIdType.MESH


class Exchange:
    def __init__(self, axis, count, scatter, stride=1, pick=None, slot=None):
        self.axis, self.count, self.scatter, self.stride = axis, count, scatter, stride
        self.pick, self.slot = pick or (lambda ref, peer: ref.at[peer]), slot

    def place(self):
        return lax.rem(lax.axis_index(self.axis) // self.stride, self.count)

    def where(self, peer):
        index = lax.axis_index(self.axis)
        return {self.axis: index + (peer - self.place()) * self.stride}

    def shape(self, shape):
        if self.slot is not None:
            return (self.count,) + self.slot
        return shape if self.scatter else (self.count,) + shape

    def scratch(self):
        return [
            pltpu.SemaphoreType.DMA,
            pltpu.SemaphoreType.DMA((self.count,)),
            pltpu.SemaphoreType.DMA((self.count,)),
        ]

    def greet(self, barrier):
        me = self.place()
        for hop in range(1, self.count):
            peer = lax.rem(me + hop, self.count)
            pl.semaphore_signal(
                barrier, inc=1, device_id=self.where(peer), device_id_type=MESH
            )
        return self.count - 1

    def start(self, x_ref, out_ref, own_sem, send_sem, recv_sem):
        me = self.place()
        own = self.pick(x_ref, me) if self.scatter else x_ref
        self.copies = [pltpu.make_async_copy(own, out_ref.at[me], own_sem)]
        for hop in range(1, self.count):
            peer = lax.rem(me + hop, self.count)
            self.copies.append(
                pltpu.make_async_remote_copy(
                    src_ref=self.pick(x_ref, peer) if self.scatter else x_ref,
                    dst_ref=out_ref.at[me],
                    send_sem=send_sem.at[hop],
                    recv_sem=recv_sem.at[hop],
                    device_id=self.where(peer),
                    device_id_type=MESH,
                )
            )
        for copy in self.copies[1:]:
            copy.start()
        self.copies[0].start()

    def finish(self, *refs):
        for copy in self.copies:
            copy.wait()


class Spread:
    def __init__(self, sends, takes, n_sends, n_takes):
        self.sends, self.takes, self.n_sends, self.n_takes = sends, takes, n_sends, n_takes

    def shape(self, shape):
        return (self.n_takes,) + shape

    def scratch(self):
        return [
            pltpu.SemaphoreType.DMA,
            pltpu.SemaphoreType.DMA((self.n_sends,)),
            pltpu.SemaphoreType.DMA((self.n_takes,)),
        ]

    def greet(self, barrier):
        for where in self.takes((lax.axis_index("fsdp"), lax.axis_index("tp"))):
            pl.semaphore_signal(barrier, inc=1, device_id=where, device_id_type=MESH)
        return self.n_sends

    def each(self, pairs, remote, local):
        me = (lax.axis_index("fsdp"), lax.axis_index("tp"))
        for index, (where, slot) in enumerate(pairs(me)):
            other = jnp.logical_or(where[0] != me[0], where[1] != me[1])

            @pl.when(other)
            def _():
                remote(index, where, slot)

            if local is not None:

                @pl.when(jnp.logical_not(other))
                def _():
                    local(slot)

    def start(self, x_ref, out_ref, own_sem, send_sem, recv_sem):
        def copy(index, where, slot):
            return pltpu.make_async_remote_copy(
                src_ref=x_ref,
                dst_ref=out_ref.at[slot],
                send_sem=send_sem.at[index],
                recv_sem=recv_sem.at[slot],
                device_id=where,
                device_id_type=MESH,
            )

        self.copy = copy
        self.each(
            self.sends,
            lambda *at: copy(*at).start(),
            lambda slot: pltpu.make_async_copy(x_ref, out_ref.at[slot], own_sem).start(),
        )

    def finish(self, x_ref, out_ref, own_sem, send_sem, recv_sem):
        self.each(
            lambda me: [(where, slot) for slot, where in enumerate(self.takes(me))],
            lambda index, where, slot: self.copy(0, where, slot).wait_recv(),
            lambda slot: pltpu.make_async_copy(x_ref, out_ref.at[slot], own_sem).wait(),
        )
        self.each(self.sends, lambda *at: self.copy(*at).wait_send(), None)


class Chain:
    def __init__(self, count, per, parts):
        self.count, self.per, self.parts = count, per, parts

    def shape(self, shape):
        return shape[:1] + (self.per,) + shape[1:]

    def scratch(self):
        pieces = self.pieces
        return [
            pltpu.SemaphoreType.DMA((pieces,)),
            pltpu.SemaphoreType.DMA((2, pieces)),
            pltpu.SemaphoreType.DMA((pieces,)),
            pltpu.SemaphoreType.DMA((self.per, pieces)),
            pltpu.SemaphoreType.DMA((self.per, pieces)),
        ]

    @property
    def pieces(self):
        return 2 * self.parts

    def places(self):
        me = lax.axis_index("fsdp")
        return me // self.per, lax.rem(me, self.per)

    def mates(self):
        group, spot = self.places()
        return [
            {"fsdp": group * self.per + lax.rem(spot + hop, self.per)}
            for hop in range(1, self.per)
        ]

    def beside(self, step):
        group, spot = self.places()
        return {"fsdp": lax.rem(group + step + self.count, self.count) * self.per + spot}

    def greet(self, barrier):
        for where in self.mates() + [self.beside(1), self.beside(-1)]:
            pl.semaphore_signal(barrier, inc=1, device_id=where, device_id_type=MESH)
        return self.per + 1

    def start(self, x_ref, out_ref, own_sem, pass_sem, come_sem, swap_sem, meet_sem):
        group, spot = self.places()
        source = lax.axis_index("tp")
        size = x_ref.shape[1] // self.parts

        def at(piece, owner):
            mat, part = piece // self.parts, piece % self.parts
            return out_ref.at[mat, owner, pl.ds(part * size, size)]

        def own(piece):
            mat, part = piece // self.parts, piece % self.parts
            return pltpu.make_async_copy(
                x_ref.at[mat, pl.ds(part * size, size)], at(piece, spot), own_sem.at[piece]
            )

        def along(piece, way):
            return pltpu.make_async_remote_copy(
                src_ref=at(piece, spot),
                dst_ref=at(piece, spot),
                send_sem=pass_sem.at[way, piece],
                recv_sem=come_sem.at[piece],
                device_id=self.beside(1 if way == 0 else -1),
                device_id_type=MESH,
            )

        def swap(piece, hop):
            return pltpu.make_async_remote_copy(
                src_ref=at(piece, spot),
                dst_ref=at(piece, spot),
                send_sem=swap_sem.at[hop, piece],
                recv_sem=meet_sem.at[hop, piece],
                device_id=self.mates()[hop - 1],
                device_id_type=MESH,
            )

        onward = (
            jnp.logical_and(group >= source, group < self.count - 1),
            jnp.logical_and(group <= source, group > 0),
        )

        @pl.when(group == source)
        def _():
            for piece in range(self.pieces):
                own(piece).start()

        for piece in range(self.pieces):

            @pl.when(group == source)
            def _():
                own(piece).wait()

            @pl.when(group != source)
            def _():
                along(piece, 0).wait_recv()

            for way in range(2):

                @pl.when(onward[way])
                def _():
                    along(piece, way).start()

            for hop in range(1, self.per):
                swap(piece, hop).start()

        for piece in range(self.pieces):
            for hop in range(1, self.per):
                swap(piece, hop).wait()
            for way in range(2):

                @pl.when(onward[way])
                def _():
                    along(piece, way).wait_send()

    def finish(self, *refs):
        pass


def transfer_kernel(moves, *refs):
    count = len(moves)
    sems, spans = list(refs[2 * count :]), []
    for index, move in enumerate(moves):
        held = len(move.scratch())
        spans.append((refs[index], refs[count + index], *sems[:held]))
        sems = sems[held:]
    barrier = pltpu.get_barrier_semaphore()
    pl.semaphore_wait(barrier, sum(move.greet(barrier) for move in moves))
    for move, span in zip(moves, spans):
        move.start(*span)
    for move, span in zip(moves, spans):
        move.finish(*span)


def transfer(ident, *pairs):
    values, moves = [pair[0] for pair in pairs], [pair[1] for pair in pairs]
    results = pl.pallas_call(
        functools.partial(transfer_kernel, moves),
        out_shape=[
            jax.ShapeDtypeStruct(move.shape(value.shape), value.dtype)
            for value, move in zip(values, moves)
        ],
        in_specs=[pl.BlockSpec(memory_space=pl.ANY)] * len(values),
        out_specs=[pl.BlockSpec(memory_space=pl.ANY)] * len(values),
        scratch_shapes=[sem for move in moves for sem in move.scratch()],
        compiler_params=pltpu.CompilerParams(collective_id=ident, has_side_effects=True),
    )(*values)
    return results[0] if len(results) == 1 else results


def halves(value):
    head = lax.reduce_precision(value, 8, 7)
    return head.astype(jnp.bfloat16), (value - head).astype(jnp.bfloat16)


def mixed(form, exact, value):
    head, tail = halves(value)
    dot = functools.partial(jnp.einsum, form, preferred_element_type=jnp.float32)
    return dot(exact, head) + dot(exact, tail)


def orthogonal_mix(raw):
    rank = raw.shape[-1]
    eye = jnp.eye(rank, dtype=jnp.float32)
    scale = (jnp.sqrt(jnp.sum(raw * eye, axis=(1, 2))) + NORM_EPS)[:, None, None]
    gram = raw / scale / scale
    mul = functools.partial(jnp.einsum, "mkl,mlj->mkj", precision=HIGH)
    total = None
    for step in range(NS_STEPS):
        mixer = COEF_A * eye + COEF_B * gram + COEF_C * mul(gram, gram)
        total = mixer if total is None else mul(total, mixer)
        if step < NS_STEPS - 1:
            gram = mul(mul(mixer, gram), mixer)
    return total, scale


def body(nf, nt, activations, out_grads, bases, weights, first_moment, second_moment):
    tokens, feats = activations.shape
    mats, rows, rank = bases.shape
    slab = mats * rank // nt
    per = feats // rows
    mine_f, mine_t = lax.axis_index("fsdp"), lax.axis_index("tp")

    outs, own_bases = transfer(
        0,
        (jnp.stack([out_grads[j * mats // nt] for j in range(nt)]), Exchange("tp", nt, True)),
        (bases, Chain(nf // per, per, 8)),
    )
    own_bases = own_bases.reshape(mats, feats, rank)

    part = mixed("tf,mfk->mtk", activations, own_bases)
    part = part.reshape(mats, tokens, nt // mats, slab)
    part = jnp.transpose(part, (0, 2, 1, 3)).reshape(nt, tokens, slab)
    along = jnp.sum(transfer(1, (part, Exchange("tp", nt, True))), axis=0)

    part = mixed("jtc,tk->kjc", outs, along).reshape(nf, -1, nt * outs.shape[2])
    part = jnp.sum(transfer(2, (part, Exchange("fsdp", nf, True))), axis=0)
    proj = transfer(3, (part, Exchange("fsdp", nf, False))).reshape(slab, nt, -1)

    rank_rows = first_moment.shape[1]
    picked = lax.dynamic_slice_in_dim(proj, lax.rem(mine_f * rank_rows, slab), rank_rows, 0)
    back = mixed("jtc,kjc->tk", outs, proj)
    back, picked = transfer(
        4,
        (back, Exchange("tp", nt, False)),
        (jnp.transpose(picked, (1, 0, 2)), Exchange("tp", nt, True)),
    )

    spot = mine_f * rank_rows // slab
    own_proj = jnp.stack(
        [lax.dynamic_index_in_dim(picked, m * (nt // mats) + spot, 0, False) for m in range(mats)]
    )
    new_first = BETA_ONE * first_moment + (1.0 - BETA_ONE) * own_proj
    new_second = BETA_TWO * second_moment + (1.0 - BETA_TWO) * own_proj * own_proj
    adam_step = new_first / CORRECT_ONE / (jnp.sqrt(new_second / CORRECT_TWO) + EPSILON)

    groups = nf // per
    width = mats * rank
    back = jnp.transpose(back, (1, 0, 2)).reshape(tokens, width)
    part = mixed("tf,tk->fk", activations, back).reshape(groups, per, -1, width)
    depth = part.shape[2]
    upper = depth * 11 // 16 // 8 * 8
    lower = depth - upper
    near, far = transfer(
        5,
        (part, Exchange("fsdp", per, True, 1,
                        lambda ref, peer: ref.at[:, peer, pl.ds(0, upper)], (groups, upper, width))),
        (part, Exchange("fsdp", groups, True, per,
                        lambda ref, peer: ref.at[peer, :, pl.ds(upper, lower)], (per, lower, width))),
    )
    near, far = transfer(
        9,
        (jnp.sum(near, axis=0), Exchange("fsdp", groups, True, per)),
        (jnp.sum(far, axis=0), Exchange("fsdp", per, True)),
    )
    cand = jnp.concatenate([jnp.sum(near, axis=0), jnp.sum(far, axis=0)])

    def cand_sends(me):
        flat = me[1] * nf + me[0]
        return [((flat // nt, lax.rem(flat, nt)), 0)]

    def cand_takes(me):
        flat = me[0] * nt + me[1]
        return [(lax.rem(flat, nf), flat // nf)]

    raw = cand.reshape(-1, mats, rank)
    raw = jnp.einsum("dmk,dml->mkl", raw, raw, precision=HIGH).reshape(nf, -1, rank)
    raw, cand = transfer(
        6,
        (raw, Exchange("fsdp", nf, True)),
        (cand, Spread(cand_sends, cand_takes, 1, 1)),
    )
    raw = jnp.sum(raw, axis=0)
    raw, cand, step_full = transfer(
        7,
        (raw, Exchange("tp", nt, False)),
        (cand[0], Exchange("tp", nt, False)),
        (adam_step, Exchange("fsdp", nf, False)),
    )
    step_full = jnp.transpose(step_full, (1, 0, 2, 3)).reshape(mats, rank, -1)
    new_weights = weights - RATE * jnp.einsum("mdk,mkc->mdc", bases, step_full, precision=HIGH)
    cand = cand.reshape(rows, mats, rank)
    raw = jnp.sum(raw, axis=0)
    raw = transfer(8, (raw, Exchange("fsdp", nf, False))).reshape(mats, rank, rank)
    mixer, scale = orthogonal_mix(raw)
    new_bases = jnp.einsum("dmk,mkl->mdl", cand, mixer, precision=HIGH) / scale
    return (new_weights, new_first, new_second, new_bases)


def solution(mesh):
    return jax.shard_map(
        functools.partial(body, mesh.shape["fsdp"], mesh.shape["tp"]),
        mesh=mesh,
        in_specs=(
            P("fsdp", "tp"),
            P(None, "fsdp", "tp"),
            P(None, "fsdp", None),
            P(None, "fsdp", "tp"),
            P(None, "fsdp", "tp"),
            P(None, "fsdp", "tp"),
        ),
        out_specs=(
            P(None, "fsdp", "tp"),
            P(None, "fsdp", "tp"),
            P(None, "fsdp", "tp"),
            P(None, "fsdp", None),
        ),
        check_vma=False,
    )
```
